32 devices in a mesh: seq: 2 (over core), ctx: 4 (over y, x), fsdp: 4 (over z).
Axes of the slice: x: 2, y: 2, z: 4, core: 2. Of those that a mesh axis runs over, the one named last changes fastest.
Arguments:
- tokens: bfloat16 [2, 2048, 768], P('seq', ('ctx', 'fsdp')), may hold values from -6 to 6
- documents: int32 [2, 2048], P('seq', ('ctx', 'fsdp')), may hold values from 0 to 1, as said below
- joint_weight: bfloat16 [768, 2304], P(('seq', 'fsdp')), may hold values from -0.21875 to 0.21875
- query_bias: bfloat16 [768], P(('seq', 'fsdp')), may hold values from -0.59765625 to 0.59765625
- value_bias: bfloat16 [768], P(('seq', 'fsdp')), may hold values from -0.119628906 to 0.119628906
- mixer_weight: bfloat16 [768, 768], P(('seq', 'fsdp')), may hold values from -4 to 4
- mixer_bias: bfloat16 [768], P(('seq', 'fsdp')), may hold values from -0.59765625 to 0.59765625
- first_gain: bfloat16 [768], P(('seq', 'fsdp')), may hold values from 0.5 to 1.5
- first_bias: bfloat16 [768], P(('seq', 'fsdp')), may hold values from -0.59765625 to 0.59765625
- hidden_weight: bfloat16 [768, 3072], P(('seq', 'fsdp')), may hold values from -0.21875 to 0.21875
- hidden_bias: bfloat16 [3072], P(('seq', 'fsdp')), may hold values from -0.59765625 to 0.59765625
- return_weight: bfloat16 [3072, 768], P(('seq', 'fsdp')), may hold values from -0.109375 to 0.109375
- return_bias: bfloat16 [768], P(('seq', 'fsdp')), may hold values from -0.59765625 to 0.59765625
- second_gain: bfloat16 [768], P(('seq', 'fsdp')), may hold values from 0.5 to 1.5
- second_bias: bfloat16 [768], P(('seq', 'fsdp')), may hold values from -0.59765625 to 0.59765625
- cotangent: bfloat16 [2, 2048, 768], P('seq', ('ctx', 'fsdp')), may hold values from -6 to 6
Outputs:
- result: bfloat16 [2, 2048, 768], P('seq', ('ctx', 'fsdp'))
- tokens_grad: float32 [2, 2048, 768], P('seq', ('ctx', 'fsdp'))
- joint_grad: float32 [768, 2304], P(('seq', 'fsdp'))
- query_grad: float32 [768], P(('seq', 'fsdp'))
- value_grad: float32 [768], P(('seq', 'fsdp'))
- mixer_grad: float32 [768, 768], P(('seq', 'fsdp'))
- mixer_drift: float32 [768], P(('seq', 'fsdp'))
- first_scale: float32 [768], P(('seq', 'fsdp'))
- first_drift: float32 [768], P(('seq', 'fsdp'))
- hidden_grad: float32 [768, 3072], P(('seq', 'fsdp'))
- hidden_drift: float32 [3072], P(('seq', 'fsdp'))
- return_grad: float32 [3072, 768], P(('seq', 'fsdp'))
- return_drift: float32 [768], P(('seq', 'fsdp'))
- second_scale: float32 [768], P(('seq', 'fsdp'))
- second_drift: float32 [768], P(('seq', 'fsdp'))
The draws below stay inside these ranges and needn't reach their ends.
Inputs may be any that keep to these rules, and one draw needn't show every extreme that they name: Along each sequence the document numbers start at 0 on the first token and rise by one at each new document; every sequence holds 2 documents. Each sequence holds one document of exactly 1536 tokens that starts at a multiple of 512; every other document has at most 896 tokens.
All inputs are finite; a program needn't handle non-finite values.
Results may differ from the reference program's by a relative error of at most 0.02.
Values may be sent and summed in bfloat16 or wider, within the bound.
A program may use at most 256 MiB of HBM per device.

```python
from functools import partial
import jax
import jax.numpy as jnp
from jax import lax

D = 768
HEADS = 12
HEAD_DIM = 64
FF = 3072
TOK_DEV = 128
SEQS = 2
SEQLEN = 2048
DOCS = 4
LONGDOC = 1536


def draw_documents(key, part):
    stride = 4 * TOK_DEV
    jitter = 3 * TOK_DEV // 2
    positions = jnp.arange(SEQLEN, dtype=jnp.int32)
    markers = jnp.arange(DOCS - 1, dtype=jnp.int32)
    places = DOCS // 2
    sequences = []
    for number in range(SEQS):
        folded = jax.random.fold_in(key, 11 + number)
        shifts = jax.random.randint(jax.random.fold_in(folded, 1), (DOCS - 1,), -jitter, jitter + 1, dtype=jnp.int32)
        long_place = jax.random.randint(jax.random.fold_in(folded, 2), (), 0, places, dtype=jnp.int32)
        long_start = long_place * stride
        long_end = long_start + LONGDOC
        limits = (markers + 1) * stride + shifts
        places_of = markers + 1
        inside = (places_of >= long_place) & (places_of <= long_place + DOCS // 2 + 1)
        counted = (positions[:, None] >= limits[None, :]) & jnp.logical_not(inside)[None, :]
        doc_ids = jnp.sum(counted.astype(jnp.int32), axis=1)
        doc_ids = doc_ids + ((positions >= long_start) & (long_start > 0)).astype(jnp.int32)
        doc_ids = doc_ids + ((positions >= long_end) & (long_end < SEQLEN)).astype(jnp.int32)
        sequences.append(doc_ids.astype(jnp.int32))
    return jnp.stack(sequences, 0)


def block_levels(stream_key, extent, pieces, smallest, top_value):
    level = 1.0
    for position, blocks in pieces:
        heights = jax.random.uniform(jax.random.fold_in(jax.random.fold_in(stream_key, 6), position), (blocks,), jnp.float32, smallest / len(pieces), top_value / len(pieces))
        level = level * jnp.repeat(jnp.exp(heights), extent[position] // blocks).reshape((-1,) + (1,) * (len(extent) - 1 - position))
    return level


def scatter_about(own_key, dims, width, limit, pieces=(), kind=jnp.bfloat16):
    values = jax.random.normal(own_key, dims, jnp.float32) * width
    if len(pieces) > 0:
        values = block_levels(own_key, dims, pieces, -0.22, 0.18) * values
    return jnp.clip(values, min=-limit, max=limit).astype(kind)


def setup_inputs(seed: int = 0) -> dict:
    key_list = jax.random.split(jax.random.key(seed), 17)
    tokens = scatter_about(key_list[0], (SEQS, SEQLEN, D), 1.0, 6.0, ((0, 2), (1, 16)))
    documents = draw_documents(jax.random.fold_in(key_list[16], 71), 0)
    joint_weight = scatter_about(key_list[2], (D, 3 * D), D ** -0.5, 0.21875, ((0, 8),))
    query_bias = scatter_about(key_list[3], (D,), 0.1, 0.59765625, ((0, 8),))
    value_bias = scatter_about(key_list[4], (D,), 0.02, 0.119628906, ((0, 8),))
    mixer_weight = scatter_about(key_list[5], (D, D), (max(D // 384, 1)) ** -0.5, 4.0, ((0, 8),))
    mixer_bias = scatter_about(key_list[6], (D,), 0.1, 0.59765625, ((0, 8),))
    first_gain = jnp.clip(1.0 + 0.1 * jax.random.normal(key_list[7], (D,), jnp.float32), 0.5, 1.5).astype(jnp.bfloat16)
    first_bias = scatter_about(key_list[8], (D,), 0.1, 0.59765625, ((0, 8),))
    hidden_weight = scatter_about(key_list[9], (D, FF), D ** -0.5, 0.21875, ((0, 8),))
    hidden_bias = scatter_about(key_list[10], (FF,), 0.1, 0.59765625, ((0, 8),))
    return_weight = scatter_about(key_list[11], (FF, D), FF ** -0.5, 0.109375, ((0, 8),))
    return_bias = scatter_about(key_list[12], (D,), 0.1, 0.59765625, ((0, 8),))
    second_gain = jnp.clip(1.0 + 0.1 * jax.random.normal(key_list[13], (D,), jnp.float32), 0.5, 1.5).astype(jnp.bfloat16)
    second_bias = scatter_about(key_list[14], (D,), 0.1, 0.59765625, ((0, 8),))
    cotangent = scatter_about(key_list[15], (SEQS, SEQLEN, D), 1.0, 6.0, ((0, 2), (1, 16)))
    return dict(tokens=tokens, documents=documents, joint_weight=joint_weight, query_bias=query_bias, value_bias=value_bias, mixer_weight=mixer_weight, mixer_bias=mixer_bias, first_gain=first_gain, first_bias=first_bias, hidden_weight=hidden_weight, hidden_bias=hidden_bias, return_weight=return_weight, return_bias=return_bias, second_gain=second_gain, second_bias=second_bias, cotangent=cotangent)


highest = lax.Precision.HIGHEST

@jax.custom_vjp
def low(v):
    return lax.optimization_barrier(v.astype(jnp.bfloat16)).astype(jnp.float32)

@jax.custom_vjp
def low_back(v):
    return v

def low_keep(v):
    return (low(v), None)

def low_pass(kept, grad):
    return (grad,)

def back_keep(v):
    return (v, None)

def back_low(kept, grad):
    return (low(grad),)
low.defvjp(low_keep, low_pass)
low_back.defvjp(back_keep, back_low)

def matmul(operand, matrix):
    return jnp.dot(operand, matrix, precision=highest)

def layer_norm(values, gain, shift):
    center = values - lax.optimization_barrier(jnp.mean(values, axis=-1, keepdims=True))
    inverse = lax.rsqrt(lax.optimization_barrier(jnp.mean(center * center, axis=-1, keepdims=True)) + 1e-06)
    return center * inverse * gain + shift

def attend(query_all, key_all, value_all, doc_ids):
    factor = float(HEAD_DIM) ** (-0.5)
    blocks = 8
    block_rows = SEQLEN // blocks
    query_blocks = query_all.reshape(SEQS * blocks, block_rows, HEADS, HEAD_DIM)
    doc_blocks = doc_ids.reshape(SEQS * blocks, block_rows)
    holders = (jnp.arange(SEQS * blocks, dtype=jnp.int32) // blocks).astype(jnp.int32)

    def one_block(packed):
        query_rows, doc_rows, holder = packed
        key_seq = lax.dynamic_index_in_dim(key_all, holder, 0, keepdims=False)
        value_seq = lax.dynamic_index_in_dim(value_all, holder, 0, keepdims=False)
        doc_cols = lax.dynamic_index_in_dim(doc_ids, holder, 0, keepdims=False)
        scores = low_back(jnp.einsum('qhd,khd->hqk', query_rows, key_seq, precision=highest) * factor)
        allowed = (doc_rows[:, None] == doc_cols[None, :])[None]
        masked = jnp.where(allowed, scores, -1e+30)
        row_peak = lax.optimization_barrier(jnp.max(masked, axis=-1, keepdims=True))
        weights = jnp.where(allowed, jnp.exp(masked - row_peak), 0.0)
        row_total = lax.optimization_barrier(jnp.sum(weights, axis=-1))
        blended = jnp.einsum('hqk,khd->qhd', low(weights), value_seq, precision=highest)
        return blended / jnp.transpose(row_total)[:, :, None]
    outcome = lax.map(jax.checkpoint(one_block), (query_blocks, doc_blocks, holders))
    return outcome.reshape(SEQS, SEQLEN, HEADS * HEAD_DIM)

def forward(doc_ids, inputs, joint_mat, query_add, value_add, mixer_mat, mixer_add, gain_one, bias_one, hidden_mat, hidden_add, return_mat, return_add, gain_two, bias_two):
    projected = matmul(inputs, joint_mat)
    queries = low_back(low(projected[..., :D] + query_add))
    keys_part = low_back(low(projected[..., D:2 * D]))
    values_part = low_back(low(projected[..., 2 * D:] + value_add))
    shaped = (SEQS, SEQLEN, HEADS, HEAD_DIM)
    attention = attend(queries.reshape(shaped), keys_part.reshape(shaped), values_part.reshape(shaped), doc_ids)
    attention = low_back(low(attention))
    branch = low_back(matmul(attention, mixer_mat) + mixer_add)
    first = layer_norm(inputs + branch, gain_one, bias_one)
    inner = low_back(matmul(low(first), hidden_mat) + hidden_add)
    acted = low(jax.nn.gelu(inner, approximate=False))
    second_branch = low_back(matmul(acted, return_mat) + return_add)
    return layer_norm(first + second_branch, gain_two, bias_two)

def reference(tokens, documents, joint_weight, query_bias, value_bias, mixer_weight, mixer_bias, first_gain, first_bias, hidden_weight, hidden_bias, return_weight, return_bias, second_gain, second_bias, cotangent):
    floats = [array.astype(jnp.float32) for array in (tokens, joint_weight, query_bias, value_bias, mixer_weight, mixer_bias, first_gain, first_bias, hidden_weight, hidden_bias, return_weight, return_bias, second_gain, second_bias)]
    outcome, pullback = jax.vjp(partial(forward, documents), *floats)
    grads = pullback(cotangent.astype(jnp.float32))
    return (outcome.astype(jnp.bfloat16), grads[0], grads[1], grads[2], grads[3], grads[4], grads[5], grads[6], grads[7], grads[8], grads[9], grads[10], grads[11], grads[12], grads[13])
```

```python
import functools
import math

import jax
import jax.numpy as jnp
from jax import lax
from jax.experimental import pallas as pl
from jax.experimental.pallas import tpu as pltpu
from jax.sharding import PartitionSpec as P

HEADS = 12
HEAD_DIM = 64
MESH = pl.DeviceIdType.MESH
BF = jnp.bfloat16
F32 = jnp.float32


def contract_rows(operand, other):
    return lax.dot_general(
        operand, other, (((0,), (0,)), ((), ())), preferred_element_type=jnp.float32
    )


def contract_cols(operand, other):
    return lax.dot_general(
        operand, other, (((1,), (1,)), ((), ())), preferred_element_type=jnp.float32
    )


def any_norm_forward(values, gain, shift):
    center = values - jnp.mean(values, axis=-1, keepdims=True)
    inverse = lax.rsqrt(jnp.mean(center * center, axis=-1, keepdims=True) + 1e-06)
    normed = center * inverse
    return (normed * gain + shift, normed, inverse)


def any_norm_backward(upstream, normed, inverse, gain):
    gain_grad = jnp.sum(upstream * normed, axis=0)
    shift_grad = jnp.sum(upstream, axis=0)
    scaled = upstream * gain
    plain_mean = jnp.mean(scaled, axis=-1, keepdims=True)
    cross_mean = jnp.mean(scaled * normed, axis=-1, keepdims=True)
    return (inverse * (scaled - plain_mean - normed * cross_mean), gain_grad, shift_grad)


def gelu_exact(values):
    return jax.nn.gelu(values, approximate=False)


def by_blocks(step_fn, running, incoming, tok_rows):
    row_count = incoming[0].shape[0]
    shard_count = row_count // tok_rows
    limit_shards = max(1, 1024 // tok_rows)
    group_size = math.gcd(shard_count, 1 << limit_shards.bit_length() - 1)
    block_rows = group_size * tok_rows
    turn_count = row_count // block_rows
    stacked = tuple(
        (member.reshape((turn_count, block_rows) + member.shape[1:]) for member in incoming)
    )

    def scan_step(current, element):
        portion, number = element
        return (step_fn(current, portion, number * block_rows), None)

    running, unused = lax.scan(
        scan_step, running, (stacked, jnp.arange(turn_count, dtype=jnp.int32))
    )
    return running


def any_shards(
    tokens,
    documents,
    joint_weight,
    query_bias,
    value_bias,
    mixer_weight,
    mixer_bias,
    first_gain,
    first_bias,
    hidden_weight,
    hidden_bias,
    return_weight,
    return_bias,
    second_gain,
    second_bias,
    cotangent,
):
    inputs = tokens[0]
    tok_rows = inputs.shape[0]
    model_width = inputs.shape[1]
    factor = float(HEAD_DIM) ** (-0.5)
    joint_full, mixer_full, query_full, value_full, offset_full, gain_first, bias_first = (
        lax.all_gather(joint_weight, ("seq", "fsdp"), axis=0, tiled=True),
        lax.all_gather(mixer_weight, ("seq", "fsdp"), axis=0, tiled=True),
        lax.all_gather(query_bias, ("seq", "fsdp"), axis=0, tiled=True),
        lax.all_gather(value_bias, ("seq", "fsdp"), axis=0, tiled=True),
        lax.all_gather(mixer_bias, ("seq", "fsdp"), axis=0, tiled=True),
        lax.all_gather(first_gain, ("seq", "fsdp"), axis=0, tiled=True),
        lax.all_gather(first_bias, ("seq", "fsdp"), axis=0, tiled=True),
    )
    projected = jnp.dot(inputs, joint_full, preferred_element_type=jnp.float32)
    queries = (projected[:, :model_width] + query_full.astype(jnp.float32)).astype(jnp.bfloat16)
    keys_loc = projected[:, model_width : 2 * model_width].astype(jnp.bfloat16)
    values_loc = (projected[:, 2 * model_width :] + value_full.astype(jnp.float32)).astype(
        jnp.bfloat16
    )
    doc_rows = documents[0].astype(jnp.float32) + 1.0
    doc_send = doc_rows.astype(jnp.bfloat16)
    query_heads = queries.reshape(tok_rows, HEADS, HEAD_DIM)
    key_heads = keys_loc.reshape(tok_rows, HEADS, HEAD_DIM)
    value_heads = values_loc.reshape(tok_rows, HEADS, HEAD_DIM)

    def forward_step(running, incoming, offset):
        peak_old, total_old, weighted_old = running
        key_piece, value_piece, doc_piece = incoming
        row_count = key_piece.shape[0]
        key_split = key_piece.reshape(row_count, HEADS, HEAD_DIM)
        value_split = value_piece.reshape(row_count, HEADS, HEAD_DIM)
        scores = (
            jnp.einsum("qhd,khd->hqk", query_heads, key_split, preferred_element_type=jnp.float32)
            * factor
        )
        allowed = (doc_rows[:, None] == doc_piece.astype(jnp.float32)[None, :])[None]
        masked = jnp.where(allowed, scores, -1e30)
        peak_new = jnp.maximum(peak_old, jnp.max(masked, axis=-1))
        weights = jnp.where(allowed, jnp.exp(masked - peak_new[:, :, None]), 0.0)
        rescale = jnp.exp(peak_old - peak_new)
        total_new = total_old * rescale + jnp.sum(weights, axis=-1)
        blended = jnp.einsum(
            "hqk,khd->qhd",
            weights.astype(jnp.bfloat16),
            value_split,
            preferred_element_type=jnp.float32,
        )
        weighted_new = (
            weighted_old.reshape(tok_rows, HEADS, HEAD_DIM) * jnp.transpose(rescale)[:, :, None]
            + blended
        )
        return (peak_new, total_new, weighted_new.reshape(tok_rows, model_width))

    start_fwd = (
        jnp.full((HEADS, tok_rows), -1e30, jnp.float32),
        jnp.zeros((HEADS, tok_rows), jnp.float32),
        jnp.zeros((tok_rows, model_width), jnp.float32),
    )
    row_peak, row_total, weighted = by_blocks(
        forward_step,
        start_fwd,
        (
            lax.all_gather(keys_loc, ("ctx", "fsdp"), axis=0, tiled=True),
            lax.all_gather(values_loc, ("ctx", "fsdp"), axis=0, tiled=True),
            lax.all_gather(doc_send, ("ctx", "fsdp"), axis=0, tiled=True),
        ),
        tok_rows,
    )
    attention = (
        weighted.reshape(tok_rows, HEADS, HEAD_DIM) / jnp.transpose(row_total)[:, :, None]
    ).reshape(tok_rows, model_width)
    mixed_low = attention.astype(jnp.bfloat16)
    log_total = row_peak + jnp.log(row_total)
    branch = jnp.dot(
        mixed_low, mixer_full, preferred_element_type=jnp.float32
    ) + offset_full.astype(jnp.float32)
    first_norm, first_hat, first_inv = any_norm_forward(
        inputs.astype(jnp.float32) + branch,
        gain_first.astype(jnp.float32),
        bias_first.astype(jnp.float32),
    )
    hidden_full, return_full, inner_shift, outer_shift, gain_second, bias_second = (
        lax.all_gather(hidden_weight, ("seq", "fsdp"), axis=0, tiled=True),
        lax.all_gather(return_weight, ("seq", "fsdp"), axis=0, tiled=True),
        lax.all_gather(hidden_bias, ("seq", "fsdp"), axis=0, tiled=True),
        lax.all_gather(return_bias, ("seq", "fsdp"), axis=0, tiled=True),
        lax.all_gather(second_gain, ("seq", "fsdp"), axis=0, tiled=True),
        lax.all_gather(second_bias, ("seq", "fsdp"), axis=0, tiled=True),
    )
    first_low = first_norm.astype(jnp.bfloat16)
    inner = jnp.dot(
        first_low, hidden_full, preferred_element_type=jnp.float32
    ) + inner_shift.astype(jnp.float32)
    acted, gelu_pull = jax.vjp(gelu_exact, inner)
    acted_low = acted.astype(jnp.bfloat16)
    second_in = (
        first_norm
        + jnp.dot(acted_low, return_full, preferred_element_type=jnp.float32)
        + outer_shift.astype(jnp.float32)
    )
    outcome, second_hat, second_inv = any_norm_forward(
        second_in, gain_second.astype(jnp.float32), bias_second.astype(jnp.float32)
    )
    upstream = cotangent[0].astype(jnp.float32)
    back_second, second_scale, second_drift = any_norm_backward(
        upstream, second_hat, second_inv, gain_second.astype(jnp.float32)
    )
    back_return = back_second.astype(jnp.bfloat16)
    return_drift = jnp.sum(back_return.astype(jnp.float32), axis=0)
    return_grad = contract_rows(acted_low, back_return)
    back_inner = gelu_pull(contract_cols(back_return, return_full))[0].astype(jnp.bfloat16)
    hidden_drift = jnp.sum(back_inner.astype(jnp.float32), axis=0)
    hidden_grad = contract_rows(first_low, back_inner)
    back_first = back_second + contract_cols(back_inner, hidden_full)
    back_first_in, first_scale, first_drift = any_norm_backward(
        back_first, first_hat, first_inv, gain_first.astype(jnp.float32)
    )
    back_mix = back_first_in.astype(jnp.bfloat16)
    mixer_drift = jnp.sum(back_mix.astype(jnp.float32), axis=0)
    mixer_grad = contract_rows(mixed_low, back_mix)
    back_att = contract_cols(back_mix, mixer_full).astype(jnp.bfloat16)
    delta = jnp.transpose(
        jnp.sum(
            (back_att.astype(jnp.float32) * attention).reshape(tok_rows, HEADS, HEAD_DIM), axis=-1
        )
    )
    stats_lse, stats_delta = (
        lax.all_gather(log_total, ("ctx", "fsdp"), axis=1, tiled=True),
        lax.all_gather(delta, ("ctx", "fsdp"), axis=1, tiled=True),
    )
    back_heads = back_att.reshape(tok_rows, HEADS, HEAD_DIM)

    def backward_step(running, incoming, offset):
        query_back, key_back, value_back = running
        query_piece, key_piece, value_piece, grad_piece, doc_piece = incoming
        row_count = key_piece.shape[0]
        query_split = query_piece.reshape(row_count, HEADS, HEAD_DIM)
        key_split = key_piece.reshape(row_count, HEADS, HEAD_DIM)
        value_split = value_piece.reshape(row_count, HEADS, HEAD_DIM)
        grad_split = grad_piece.reshape(row_count, HEADS, HEAD_DIM)
        lse_piece = lax.dynamic_slice_in_dim(stats_lse, offset, row_count, 1)
        delta_piece = lax.dynamic_slice_in_dim(stats_delta, offset, row_count, 1)
        allowed = doc_rows[:, None] == doc_piece.astype(jnp.float32)[None, :]
        scores = (
            jnp.einsum("qhd,khd->hqk", query_heads, key_split, preferred_element_type=jnp.float32)
            * factor
        )
        probs = jnp.where(allowed[None], jnp.exp(scores - log_total[:, :, None]), 0.0)
        dprobs = jnp.einsum(
            "qhd,khd->hqk", back_heads, value_split, preferred_element_type=jnp.float32
        )
        dscores = (probs * (dprobs - delta[:, :, None])).astype(jnp.bfloat16)
        query_back = query_back + factor * jnp.einsum(
            "hqk,khd->qhd", dscores, key_split, preferred_element_type=jnp.float32
        ).reshape(tok_rows, model_width)
        scores_rev = (
            jnp.einsum("qhd,khd->hqk", query_split, key_heads, preferred_element_type=jnp.float32)
            * factor
        )
        probs_rev = jnp.where(
            jnp.transpose(allowed)[None], jnp.exp(scores_rev - lse_piece[:, :, None]), 0.0
        )
        value_back = value_back + jnp.einsum(
            "hqk,qhd->khd",
            probs_rev.astype(jnp.bfloat16),
            grad_split,
            preferred_element_type=jnp.float32,
        ).reshape(tok_rows, model_width)
        dprobs_rev = jnp.einsum(
            "qhd,khd->hqk", grad_split, value_heads, preferred_element_type=jnp.float32
        )
        dscores_rev = (probs_rev * (dprobs_rev - delta_piece[:, :, None])).astype(jnp.bfloat16)
        key_back = key_back + factor * jnp.einsum(
            "hqk,qhd->khd", dscores_rev, query_split, preferred_element_type=jnp.float32
        ).reshape(tok_rows, model_width)
        return (query_back, key_back, value_back)

    start_back = (
        jnp.zeros((tok_rows, model_width), jnp.float32),
        jnp.zeros((tok_rows, model_width), jnp.float32),
        jnp.zeros((tok_rows, model_width), jnp.float32),
    )
    query_back, key_back, value_back = by_blocks(
        backward_step,
        start_back,
        (
            lax.all_gather(queries, ("ctx", "fsdp"), axis=0, tiled=True),
            lax.all_gather(keys_loc, ("ctx", "fsdp"), axis=0, tiled=True),
            lax.all_gather(values_loc, ("ctx", "fsdp"), axis=0, tiled=True),
            lax.all_gather(back_att, ("ctx", "fsdp"), axis=0, tiled=True),
            lax.all_gather(doc_send, ("ctx", "fsdp"), axis=0, tiled=True),
        ),
        tok_rows,
    )
    proj_back = jnp.concatenate(
        [
            query_back.astype(jnp.bfloat16),
            key_back.astype(jnp.bfloat16),
            value_back.astype(jnp.bfloat16),
        ],
        axis=1,
    )
    joint_grad = contract_rows(inputs, proj_back)
    query_grad = jnp.sum(proj_back[:, :model_width].astype(jnp.float32), axis=0)
    value_grad = jnp.sum(proj_back[:, 2 * model_width :].astype(jnp.float32), axis=0)
    tokens_grad = back_first_in + contract_cols(proj_back, joint_full)
    joint_part, mixer_part, query_part, value_part, drift_part, scale_part, shift_part = (
        lax.psum_scatter(
            joint_grad.astype(jnp.bfloat16), ("seq", "fsdp"), scatter_dimension=0, tiled=True
        ).astype(jnp.float32),
        lax.psum_scatter(
            mixer_grad.astype(jnp.bfloat16), ("seq", "fsdp"), scatter_dimension=0, tiled=True
        ).astype(jnp.float32),
        lax.psum_scatter(
            query_grad.astype(jnp.bfloat16), ("seq", "fsdp"), scatter_dimension=0, tiled=True
        ).astype(jnp.float32),
        lax.psum_scatter(
            value_grad.astype(jnp.bfloat16), ("seq", "fsdp"), scatter_dimension=0, tiled=True
        ).astype(jnp.float32),
        lax.psum_scatter(
            mixer_drift.astype(jnp.bfloat16), ("seq", "fsdp"), scatter_dimension=0, tiled=True
        ).astype(jnp.float32),
        lax.psum_scatter(
            first_scale.astype(jnp.bfloat16), ("seq", "fsdp"), scatter_dimension=0, tiled=True
        ).astype(jnp.float32),
        lax.psum_scatter(
            first_drift.astype(jnp.bfloat16), ("seq", "fsdp"), scatter_dimension=0, tiled=True
        ).astype(jnp.float32),
    )
    joint_sum, mixer_sum, query_sum, value_sum, drift_sum, scale_sum, shift_sum = (
        lax.psum(joint_part.astype(jnp.bfloat16), "ctx").astype(jnp.float32),
        lax.psum(mixer_part.astype(jnp.bfloat16), "ctx").astype(jnp.float32),
        lax.psum(query_part.astype(jnp.bfloat16), "ctx").astype(jnp.float32),
        lax.psum(value_part.astype(jnp.bfloat16), "ctx").astype(jnp.float32),
        lax.psum(drift_part.astype(jnp.bfloat16), "ctx").astype(jnp.float32),
        lax.psum(scale_part.astype(jnp.bfloat16), "ctx").astype(jnp.float32),
        lax.psum(shift_part.astype(jnp.bfloat16), "ctx").astype(jnp.float32),
    )
    hidden_part, return_part, inner_part, outer_part, gain_part, bias_part = (
        lax.psum_scatter(
            hidden_grad.astype(jnp.bfloat16), ("seq", "fsdp"), scatter_dimension=0, tiled=True
        ).astype(jnp.float32),
        lax.psum_scatter(
            return_grad.astype(jnp.bfloat16), ("seq", "fsdp"), scatter_dimension=0, tiled=True
        ).astype(jnp.float32),
        lax.psum_scatter(
            hidden_drift.astype(jnp.bfloat16), ("seq", "fsdp"), scatter_dimension=0, tiled=True
        ).astype(jnp.float32),
        lax.psum_scatter(
            return_drift.astype(jnp.bfloat16), ("seq", "fsdp"), scatter_dimension=0, tiled=True
        ).astype(jnp.float32),
        lax.psum_scatter(
            second_scale.astype(jnp.bfloat16), ("seq", "fsdp"), scatter_dimension=0, tiled=True
        ).astype(jnp.float32),
        lax.psum_scatter(
            second_drift.astype(jnp.bfloat16), ("seq", "fsdp"), scatter_dimension=0, tiled=True
        ).astype(jnp.float32),
    )
    hidden_sum, return_sum, inner_sum, outer_sum, gain_sum, bias_sum = (
        lax.psum(hidden_part.astype(jnp.bfloat16), "ctx").astype(jnp.float32),
        lax.psum(return_part.astype(jnp.bfloat16), "ctx").astype(jnp.float32),
        lax.psum(inner_part.astype(jnp.bfloat16), "ctx").astype(jnp.float32),
        lax.psum(outer_part.astype(jnp.bfloat16), "ctx").astype(jnp.float32),
        lax.psum(gain_part.astype(jnp.bfloat16), "ctx").astype(jnp.float32),
        lax.psum(bias_part.astype(jnp.bfloat16), "ctx").astype(jnp.float32),
    )
    return (
        outcome[None].astype(jnp.bfloat16),
        tokens_grad[None],
        joint_sum,
        query_sum,
        value_sum,
        mixer_sum,
        drift_sum,
        scale_sum,
        shift_sum,
        hidden_sum,
        inner_sum,
        return_sum,
        outer_sum,
        gain_sum,
        bias_sum,
    )


T = 128
C = 512
HL = 3
HF = HL * HEAD_DIM
D = 768
W3 = 3 * HF
NEG = -1e30


def nn(a, b):
    return lax.dot_general(a, b, (((1,), (0,)), ((), ())), preferred_element_type=F32)


def nt(a, b):
    return lax.dot_general(a, b, (((1,), (1,)), ((), ())), preferred_element_type=F32)


def tn(a, b):
    return lax.dot_general(a, b, (((0,), (0,)), ((), ())), preferred_element_type=F32)


def flip(value, bits):
    for bit in (1, 2):
        if bits & bit:
            value = value + bit - 2 * bit * lax.rem(lax.div(value, bit), 2)
    return value


def places():
    s, c, z = lax.axis_index("seq"), lax.axis_index("ctx"), lax.axis_index("fsdp")
    plane = {k: (s, flip(c, k), z) for k in (1, 2, 3)}
    line = {k: (s, c, flip(z, k)) for k in (1, 2, 3)}
    return s, c, z, plane, line, (1 - s, c, z)


def meet(peers):
    barrier = pltpu.get_barrier_semaphore()
    for peer in peers:
        pl.semaphore_signal(barrier, inc=1, device_id=peer, device_id_type=MESH)
    pl.semaphore_wait(barrier, len(peers))


def push(src, dst, send, recv, index, peer):
    copy = pltpu.make_async_remote_copy(
        src_ref=src,
        dst_ref=dst,
        send_sem=send.at[index],
        recv_sem=recv.at[index],
        device_id=peer,
        device_id_type=MESH,
    )
    copy.start()
    return copy


def split_heads(packed, dest, slot):
    for part in range(3):
        for h in range(HL):
            lo = part * HF + h * HEAD_DIM
            dest[part][slot, h] = packed[slot, :, lo : lo + HEAD_DIM]


def attend_kernel(
    x_ref, w_ref, doc_ref,
    mixed_ref, att_ref, lse_ref, xcol_ref, wcol_ref, k_ref, v_ref, q_ref, docs_ref,
    wbuf, kvq, mix_own, m_sc, l_sc, acc_sc, doc_col,
    send_x, recv_x, send_w, recv_w, send_d, recv_d, send_c, recv_c, send_kv, recv_kv, send_q, recv_q, send_e, recv_e, send_m, recv_m,
):
    s, c, z, plane, line, twin = places()
    me = 4 * s + z
    meet([plane[1], plane[2], plane[3], line[1], line[2], line[3], twin])
    docs_ref[0, z] = doc_ref[...]
    xcol_ref[pl.ds(pl.multiple_of(z * T, T), T), :] = x_ref[...]
    mine = xcol_ref.at[pl.ds(pl.multiple_of(z * T, T), T), :]
    xs = [push(x_ref, mine, send_x, recv_x, k, line[k]) for k in (1, 2, 3)]
    ds = [push(doc_ref, docs_ref.at[0, z], send_d, recv_d, k, line[k]) for k in (1, 2, 3)]
    ws = {}
    for k in (1, 2, 3):
        ws[k] = push(w_ref.at[flip(z, k)], wbuf.at[me], send_w, recv_w, k, line[k])
    wbuf[me] = w_ref[z]
    wt = [push(wbuf.at[me], wbuf.at[me], send_c, recv_c, 0, twin)]
    for k in (1, 2, 3):
        ws[k].wait()
        slot = wbuf.at[4 * s + flip(z, k)]
        wt.append(push(slot, slot, send_c, recv_c, k, twin))
    for copy in ds:
        copy.wait()
    es = [push(docs_ref.at[0], docs_ref.at[k], send_e, recv_e, k, plane[k]) for k in (1, 2, 3)]
    for copy in xs:
        copy.wait()
    for copy in wt:
        copy.wait()
    for i in range(8):
        wcol_ref[96 * i : 96 * i + 96, :] = wbuf[i, 0:96, :]
    bias = jnp.zeros((1, W3), F32)
    for i in range(8):
        bias = bias + wbuf[i, 96:112, :].astype(F32)[0:1, :]
    for r in range(2):
        rows = slice(256 * r, 256 * r + 256)
        made = nn(xcol_ref[rows, :], wcol_ref[...]) + bias
        low = made.astype(BF)
        scaled = (low[:, 2 * HF :].astype(F32) * (1.0 / math.sqrt(HEAD_DIM))).astype(BF)
        kvq[0, rows, 0 : 2 * HF] = low[:, 0 : 2 * HF]
        kvq[0, rows, 2 * HF : W3] = scaled
        kvq[0, rows, W3:] = jnp.zeros((256, 640 - W3), BF)
    kvs = [push(kvq.at[0, :, 0 : 2 * HF], kvq.at[k, :, 0 : 2 * HF], send_kv, recv_kv, k, plane[k]) for k in (1, 2, 3)]
    qs = [push(kvq.at[0, :, 2 * HF :], kvq.at[k, :, 2 * HF :], send_q, recv_q, k, plane[k]) for k in (1, 2, 3)]
    split_heads(kvq, (k_ref, v_ref, q_ref), 0)
    for j in range(4):
        row = docs_ref[0, j, 0:1, :].astype(F32)
        doc_col[128 * j : 128 * j + 128, :] = jnp.transpose(jnp.broadcast_to(row, (T, T)))
    m_sc[...] = jnp.full(m_sc.shape, NEG, F32)
    l_sc[...] = jnp.zeros(l_sc.shape, F32)
    acc_sc[...] = jnp.zeros(acc_sc.shape, F32)
    for k in range(4):
        if k:
            es[k - 1].wait()
            kvs[k - 1].wait()
            for part, dest in enumerate((k_ref, v_ref)):
                for h in range(HL):
                    lo = part * HF + h * HEAD_DIM
                    dest[k, h] = kvq[k, :, lo : lo + HEAD_DIM]
        keys_doc = jnp.concatenate([docs_ref[k, j, 0:1, :] for j in range(4)], axis=1).astype(F32)

        def one(step, carry, k=k, keys_doc=keys_doc):
            h = lax.div(step, 2)
            rows = pl.ds(pl.multiple_of(lax.rem(step, 2) * 256, 256), 256)
            scores = nt(q_ref[0, h, rows, :], k_ref[k, h])
            allowed = doc_col[rows, 0:1] == keys_doc
            masked = jnp.where(allowed, scores, NEG)
            old = m_sc[h, rows, 0:1]
            new = jnp.maximum(old, jnp.max(masked, axis=1, keepdims=True))
            weights = jnp.where(allowed, jnp.exp(masked - new), 0.0)
            fade = jnp.exp(old - new)
            m_sc[h, rows, 0:1] = new
            l_sc[h, rows, 0:1] = l_sc[h, rows, 0:1] * fade + jnp.sum(weights, axis=1, keepdims=True)
            acc_sc[h, rows, :] = acc_sc[h, rows, :] * fade + nn(weights.astype(BF), v_ref[k, h])
            return carry

        lax.fori_loop(0, 2 * HL, one, 0)
    lane = lax.broadcasted_iota(jnp.int32, (C, T), 1)
    stats = jnp.zeros((C, T), F32)
    for h in range(HL):
        total = l_sc[h, :, 0:1]
        part = acc_sc[h] / total
        att_ref[:, h * HEAD_DIM : (h + 1) * HEAD_DIM] = part
        mix_own[:, h * HEAD_DIM : (h + 1) * HEAD_DIM] = part.astype(BF)
        stats = jnp.where(lane == h, m_sc[h, :, 0:1] + jnp.log(total), stats)
    lse_ref[...] = stats
    ms = []
    for k in (1, 2, 3):
        rows = pl.ds(pl.multiple_of(flip(z, k) * T, T), T)
        ms.append(push(mix_own.at[rows, :], mixed_ref.at[z], send_m, recv_m, k, line[k]))
    mixed_ref[z] = mix_own[pl.ds(pl.multiple_of(z * T, T), T), :]
    for k in (1, 2, 3):
        qs[k - 1].wait()
        for h in range(HL):
            lo = 2 * HF + h * HEAD_DIM
            q_ref[k, h] = kvq[k, :, lo : lo + HEAD_DIM]
    for copy in ms:
        copy.wait()


def attend(x, w_parts, doc_rows):
    heads = jax.ShapeDtypeStruct((4, HL, C, HEAD_DIM), BF)
    vmem = pl.BlockSpec(memory_space=pltpu.VMEM)
    dma = pltpu.SemaphoreType.DMA((4,))
    return pl.pallas_call(
        attend_kernel,
        out_shape=(
            jax.ShapeDtypeStruct((4, T, HF), BF),
            jax.ShapeDtypeStruct((C, HF), F32),
            jax.ShapeDtypeStruct((C, T), F32),
            jax.ShapeDtypeStruct((C, D), BF),
            jax.ShapeDtypeStruct((D, W3), BF),
            heads,
            heads,
            heads,
            jax.ShapeDtypeStruct((4, 4, 8, T), jnp.int32),
        ),
        in_specs=[vmem] * 3,
        out_specs=(vmem,) * 9,
        scratch_shapes=[
            pltpu.VMEM((8, 112, W3), BF),
            pltpu.VMEM((4, C, 640), BF),
            pltpu.VMEM((C, HF), BF),
            pltpu.VMEM((HL, C, 128), F32),
            pltpu.VMEM((HL, C, 128), F32),
            pltpu.VMEM((HL, C, HEAD_DIM), F32),
            pltpu.VMEM((C, T), F32),
        ]
        + [dma] * 16,
        compiler_params=pltpu.CompilerParams(
            collective_id=0, has_side_effects=True, vmem_limit_bytes=50 << 20
        ),
        cost_estimate=pl.CostEstimate(flops=40_000_000_000, bytes_accessed=20_000_000, transcendentals=4_000_000),
    )(x, w_parts, doc_rows)


def norm_forward(values, gain, shift):
    center = values - jnp.mean(values, axis=-1, keepdims=True)
    inverse = lax.rsqrt(jnp.mean(center * center, axis=-1, keepdims=True) + 1e-06)
    normed = center * inverse
    return (normed * gain + shift, normed, inverse)


def norm_backward(upstream, normed, inverse, gain):
    scaled = upstream * gain
    plain_mean = jnp.mean(scaled, axis=-1, keepdims=True)
    cross_mean = jnp.mean(scaled * normed, axis=-1, keepdims=True)
    return inverse * (scaled - plain_mean - normed * cross_mean)


def total_rows(values):
    return jnp.sum(values, axis=0, keepdims=True)


MIXER_BIAS, FIRST_GAIN, FIRST_BIAS, RETURN_BIAS, SECOND_GAIN, SECOND_BIAS, HIDDEN_BIAS = range(7)


def dense_kernel(
    x_ref, mixed_ref, mixer_ref, hid_ref, ret_ref, small_ref, cot_ref,
    out_ref, bfi_ref, datt_ref, rgrad_ref, hgrad_ref, mgrad_ref, vec_ref,
    firsts, acted, slope, sent, parts, backs, inners, datt_own,
    send_f, recv_f, send_p, recv_p, send_r, recv_r, send_b, recv_b, send_a, recv_a,
):
    s, c, z, plane, line, twin = places()
    meet([plane[1], plane[2], plane[3], line[1], line[2], line[3]])

    def small(row):
        return small_ref[row : row + 1, :]

    branch = small(MIXER_BIAS)
    for j in range(4):
        branch = branch + nn(mixed_ref[j], mixer_ref[HF * j : HF * j + HF, :])
    first, hat1, inv1 = norm_forward(x_ref[...].astype(F32) + branch, small(FIRST_GAIN), small(FIRST_BIAS))
    firsts[0:T, :] = first.astype(BF)
    fs = [push(firsts.at[0:T, :], firsts.at[T * k : T * k + T, :], send_f, recv_f, k, plane[k]) for k in (1, 2, 3)]
    ps = []
    second_in = first + small(RETURN_BIAS)
    for k in range(4):
        rows = slice(T * k, T * k + T)
        if k:
            fs[k - 1].wait()
        inner = nn(firsts[rows, :], hid_ref[...]) + small(HIDDEN_BIAS)
        phi = 0.5 * (1.0 + lax.erf(inner * math.sqrt(0.5)))
        slope[rows, :] = phi + inner * (jnp.exp(-0.5 * inner * inner) * (1.0 / math.sqrt(2.0 * math.pi)))
        acted[rows, :] = (inner * phi).astype(BF)
        made = nn(acted[rows, :], ret_ref[...])
        if k:
            sent[k] = made.astype(BF)
            ps.append(push(sent.at[k], parts.at[k], send_p, recv_p, k, plane[k]))
        else:
            second_in = second_in + made
    for k in (1, 2, 3):
        ps[k - 1].wait()
        second_in = second_in + parts[k].astype(F32)
    outcome, hat2, inv2 = norm_forward(second_in, small(SECOND_GAIN), small(SECOND_BIAS))
    upstream = cot_ref[...].astype(F32)
    back_second = norm_backward(upstream, hat2, inv2, small(SECOND_GAIN))
    backs[0:T, :] = back_second.astype(BF)
    rs = [push(backs.at[0:T, :], backs.at[T * k : T * k + T, :], send_r, recv_r, k, plane[k]) for k in (1, 2, 3)]
    out_ref[...] = outcome.astype(BF)
    vec_ref[0:1, :] = total_rows(upstream * hat2)
    vec_ref[1:2, :] = total_rows(upstream)
    vec_ref[2:3, :] = total_rows(backs[0:T, :].astype(F32))
    back_first = back_second
    hidden_drift = jnp.zeros((1, D), F32)
    bs = []
    for k in range(4):
        rows = slice(T * k, T * k + T)
        if k:
            rs[k - 1].wait()
        pulled = (nt(backs[rows, :], ret_ref[...]) * slope[rows, :]).astype(BF)
        inners[rows, :] = pulled
        hidden_drift = hidden_drift + total_rows(pulled.astype(F32))
        made = nt(pulled, hid_ref[...])
        if k:
            sent[k] = made.astype(BF)
            bs.append(push(sent.at[k], parts.at[4 + k], send_b, recv_b, k, plane[k]))
        else:
            back_first = back_first + made
    rgrad_ref[...] = tn(acted[...], backs[...]).astype(BF)
    hgrad_ref[...] = tn(firsts[...], inners[...]).astype(BF)
    for k in (1, 2, 3):
        bs[k - 1].wait()
        back_first = back_first + parts[4 + k].astype(F32)
    back_first_in = norm_backward(back_first, hat1, inv1, small(FIRST_GAIN))
    back_mix = back_first_in.astype(BF)
    for j in range(4):
        datt_own[j] = nt(back_mix, mixer_ref[HF * j : HF * j + HF, :]).astype(BF)
    as_ = [push(datt_own.at[flip(z, k)], datt_ref.at[z], send_a, recv_a, k, line[k]) for k in (1, 2, 3)]
    datt_ref[z] = datt_own[z]
    bfi_ref[...] = back_first_in
    for j in range(4):
        mgrad_ref[HF * j : HF * j + HF, :] = tn(mixed_ref[j], back_mix).astype(BF)
    vec_ref[3:4, :] = total_rows(back_first * hat1)
    vec_ref[4:5, :] = total_rows(back_first)
    vec_ref[5:6, :] = total_rows(back_mix.astype(F32))
    vec_ref[6:7, :] = hidden_drift
    vec_ref[7:8, :] = jnp.zeros((1, D), F32)
    for copy in as_:
        copy.wait()


def dense(x, mixed, mixer, hid, ret, small, cot):
    vmem = pl.BlockSpec(memory_space=pltpu.VMEM)
    dma = pltpu.SemaphoreType.DMA((4,))
    square = jax.ShapeDtypeStruct((D, D), BF)
    return pl.pallas_call(
        dense_kernel,
        out_shape=(
            jax.ShapeDtypeStruct((T, D), BF),
            jax.ShapeDtypeStruct((T, D), F32),
            jax.ShapeDtypeStruct((4, T, HF), BF),
            square,
            square,
            square,
            jax.ShapeDtypeStruct((8, D), F32),
        ),
        in_specs=[vmem] * 7,
        out_specs=(vmem,) * 7,
        scratch_shapes=[
            pltpu.VMEM((4 * T, D), BF),
            pltpu.VMEM((4 * T, D), BF),
            pltpu.VMEM((4 * T, D), F32),
            pltpu.VMEM((4, T, D), BF),
            pltpu.VMEM((8, T, D), BF),
            pltpu.VMEM((4 * T, D), BF),
            pltpu.VMEM((4 * T, D), BF),
            pltpu.VMEM((4, T, HF), BF),
        ]
        + [dma] * 10,
        compiler_params=pltpu.CompilerParams(
            collective_id=1, has_side_effects=True, vmem_limit_bytes=50 << 20
        ),
        cost_estimate=pl.CostEstimate(flops=30_000_000_000, bytes_accessed=10_000_000, transcendentals=1_000_000),
    )(x, mixed, mixer, hid, ret, small, cot)


def pull_kernel(
    datt_ref, att_ref, lse_ref, k_ref, v_ref, q_ref, docs_ref, xcol_ref, wcol_ref, bfi_ref,
    tok_ref, jgrad_ref, qv_ref,
    d_own, d_all, stat, dcol, dheads, doc_col, dq, dk, dv, packed, sent, parts,
    send_d, recv_d, send_s, recv_s, send_t, recv_t,
):
    s, c, z, plane, line, twin = places()
    meet([plane[1], plane[2], plane[3], line[1], line[2], line[3]])
    for j in range(4):
        d_own[T * j : T * j + T, 0:HF] = datt_ref[j]
        row = docs_ref[0, j, 0:1, :].astype(F32)
        doc_col[128 * j : 128 * j + 128, :] = jnp.transpose(jnp.broadcast_to(row, (T, T)))
    ds = [push(d_own, d_all.at[k], send_d, recv_d, k, plane[k]) for k in (1, 2, 3)]
    lane = lax.broadcasted_iota(jnp.int32, (C, T), 1)
    stats = jnp.where(lane < HL, lse_ref[...], 0.0)
    for h in range(HL):
        cols = slice(h * HEAD_DIM, (h + 1) * HEAD_DIM)
        dheads[0, h] = d_own[:, cols]
        delta = jnp.sum(d_own[:, cols].astype(F32) * att_ref[:, cols], axis=1, keepdims=True)
        stats = jnp.where(lane == 4 + h, delta, stats)
    dcol[...] = stats
    stat[0] = jnp.transpose(stats)[0:8, :]
    ss = [push(stat.at[0], stat.at[k], send_s, recv_s, k, plane[k]) for k in (1, 2, 3)]
    dq[...] = jnp.zeros(dq.shape, F32)
    dk[...] = jnp.zeros(dk.shape, F32)
    dv[...] = jnp.zeros(dv.shape, F32)

    def doc_row(k):
        return jnp.concatenate([docs_ref[k, j, 0:1, :] for j in range(4)], axis=1).astype(F32)

    for k in range(4):
        keys_doc = doc_row(k)

        def one(step, carry, k=k, keys_doc=keys_doc):
            h = lax.div(step, 2)
            rows = pl.ds(pl.multiple_of(lax.rem(step, 2) * 256, 256), 256)
            scores = nt(q_ref[0, h, rows, :], k_ref[k, h])
            allowed = doc_col[rows, 0:1] == keys_doc
            lanes = lax.broadcasted_iota(jnp.int32, (256, T), 1)
            both = dcol[rows, :]
            lse = jnp.sum(jnp.where(lanes == h, both, 0.0), axis=1, keepdims=True)
            delta = jnp.sum(jnp.where(lanes == 4 + h, both, 0.0), axis=1, keepdims=True)
            probs = jnp.where(allowed, jnp.exp(scores - lse), 0.0)
            dprobs = nt(dheads[0, h, rows, :], v_ref[k, h])
            dscores = (probs * (dprobs - delta)).astype(BF)
            dq[h, rows, :] = dq[h, rows, :] + nn(dscores, k_ref[k, h])
            return carry

        lax.fori_loop(0, 2 * HL, one, 0)
    for k in range(4):
        if k:
            ds[k - 1].wait()
            ss[k - 1].wait()
            for h in range(HL):
                dheads[k, h] = d_all[k, :, h * HEAD_DIM : (h + 1) * HEAD_DIM]
        query_doc = doc_row(k)

        def other(step, carry, k=k, query_doc=query_doc):
            h = lax.div(step, 2)
            rows = pl.ds(pl.multiple_of(lax.rem(step, 2) * 256, 256), 256)
            scores = nt(k_ref[0, h, rows, :], q_ref[k, h])
            allowed = doc_col[rows, 0:1] == query_doc
            probs = jnp.where(allowed, jnp.exp(scores - stat[k, pl.ds(h, 1), :]), 0.0)
            dv[h, rows, :] = dv[h, rows, :] + nn(probs.astype(BF), dheads[k, h])
            dprobs = nt(v_ref[0, h, rows, :], dheads[k, h])
            dscores = (probs * (dprobs - stat[k, pl.ds(4 + h, 1), :])).astype(BF)
            dk[h, rows, :] = dk[h, rows, :] + nn(dscores, q_ref[k, h])
            return carry

        lax.fori_loop(0, 2 * HL, other, 0)
    for h in range(HL):
        lo = h * HEAD_DIM
        packed[:, lo : lo + HEAD_DIM] = dk[h].astype(BF)
        packed[:, HF + lo : HF + lo + HEAD_DIM] = dv[h].astype(BF)
        packed[:, 2 * HF + lo : 2 * HF + lo + HEAD_DIM] = (dq[h] * (1.0 / math.sqrt(HEAD_DIM))).astype(BF)
    ts = []
    for j in range(4):
        sent[j] = nt(packed[T * j : T * j + T, :], wcol_ref[...]).astype(BF)
    for k in (1, 2, 3):
        ts.append(push(sent.at[flip(z, k)], parts.at[k], send_t, recv_t, k, line[k]))
    jgrad_ref[...] = tn(xcol_ref[...], packed[...]).astype(BF)
    qv_ref[...] = jnp.broadcast_to(total_rows(packed[...].astype(F32)), (8, W3))
    rows = pl.ds(pl.multiple_of(z * T, T), T)
    made = bfi_ref[...] + nt(packed[rows, :], wcol_ref[...])
    for k in (1, 2, 3):
        ts[k - 1].wait()
        made = made + parts[k].astype(F32)
    tok_ref[...] = made


def pull(datt, att, lse, keys, values, queries, docs, xcol, wcol, bfi):
    vmem = pl.BlockSpec(memory_space=pltpu.VMEM)
    dma = pltpu.SemaphoreType.DMA((4,))
    grads = pltpu.VMEM((HL, C, HEAD_DIM), F32)
    return pl.pallas_call(
        pull_kernel,
        out_shape=(
            jax.ShapeDtypeStruct((T, D), F32),
            jax.ShapeDtypeStruct((D, W3), BF),
            jax.ShapeDtypeStruct((8, W3), F32),
        ),
        in_specs=[vmem] * 10,
        out_specs=(vmem,) * 3,
        scratch_shapes=[
            pltpu.VMEM((C, 256), BF),
            pltpu.VMEM((4, C, 256), BF),
            pltpu.VMEM((4, 8, C), F32),
            pltpu.VMEM((C, T), F32),
            pltpu.VMEM((4, HL, C, HEAD_DIM), BF),
            pltpu.VMEM((C, T), F32),
            grads,
            grads,
            grads,
            pltpu.VMEM((C, W3), BF),
            pltpu.VMEM((4, T, D), BF),
            pltpu.VMEM((4, T, D), BF),
        ]
        + [dma] * 6,
        compiler_params=pltpu.CompilerParams(
            collective_id=2, has_side_effects=True, vmem_limit_bytes=50 << 20
        ),
        cost_estimate=pl.CostEstimate(flops=60_000_000_000, bytes_accessed=10_000_000, transcendentals=8_000_000),
    )(datt, att, lse, keys, values, queries, docs, xcol, wcol, bfi)


def shards(
    tokens, documents, joint_weight, query_bias, value_bias, mixer_weight, mixer_bias, first_gain, first_bias,
    hidden_weight, hidden_bias, return_weight, return_bias, second_gain, second_bias, cotangent,
):
    s, c, z = lax.axis_index("seq"), lax.axis_index("ctx"), lax.axis_index("fsdp")
    me = 4 * s + z
    x = tokens[0]
    cols = joint_weight.reshape(96, 3, 4, HF)
    cols = jnp.stack([cols[:, 1], cols[:, 2], cols[:, 0]], axis=2)
    cols = cols.transpose(1, 0, 2, 3).reshape(4, 96, W3)
    place = (jnp.arange(8, dtype=jnp.int32) == me).astype(BF)
    vals = (place[:, None] * value_bias[None, :]).reshape(4, 1, HF)
    qrys = (place[:, None] * query_bias[None, :]).reshape(4, 1, HF)
    bias = jnp.concatenate([jnp.zeros((4, 1, HF), BF), vals, qrys], axis=2)
    w_parts = jnp.concatenate([cols, bias, jnp.zeros((4, 15, W3), BF)], axis=1)
    doc_rows = jnp.broadcast_to(documents, (8, T))
    hid_part = lax.dynamic_index_in_dim(hidden_weight.reshape(96, 8, 4, 96), c, 2, keepdims=False).reshape(96, D)
    ret_part = lax.dynamic_slice_in_dim(return_weight, 96 * c, 96, 0)
    hb_part = lax.dynamic_slice_in_dim(hidden_bias, 96 * c, 96, 0)
    smalls = jnp.stack([mixer_bias, first_gain, first_bias, return_bias, second_gain, second_bias, hb_part, hb_part])
    gather = functools.partial(lax.all_gather, axis_name=("seq", "fsdp"))
    mixer_full = gather(mixer_weight, axis=0, tiled=True)
    hid_full = gather(hid_part, axis=0, tiled=True)
    ret_full = gather(ret_part, axis=0, tiled=True)
    small_full = gather(smalls, axis=1, tiled=True).astype(F32)

    mixed, att, lse, xcol, wcol, keys, values, queries, docs = attend(x, w_parts, doc_rows)
    outcome, bfi, datt, rgrad, hgrad, mgrad, vecs = dense(
        x, mixed, mixer_full, hid_full, ret_full, small_full, cotangent[0]
    )
    tok, jgrad, qv = pull(datt, att, lse, keys, values, queries, docs, xcol, wcol, bfi)

    scatter = functools.partial(lax.psum_scatter, axis_name=("seq", "fsdp"), scatter_dimension=0, tiled=True)
    ret_sum = lax.all_gather(scatter(rgrad), "ctx", axis=0, tiled=True).astype(F32)
    hid_sum = lax.all_gather(scatter(hgrad).reshape(96, 8, 1, 96), "ctx", axis=2, tiled=True)
    hid_sum = hid_sum.astype(F32).reshape(96, 4 * D)
    mixer_sum = lax.psum(scatter(mgrad), "ctx").astype(F32)
    wide = jnp.zeros((4, D, W3), BF)
    wide = lax.dynamic_update_index_in_dim(wide, jgrad, z, 0)
    wide = wide.reshape(4, D, 3, HF).transpose(1, 2, 0, 3)
    wide = jnp.stack([wide[:, 2], wide[:, 0], wide[:, 1]], axis=1).reshape(D, 3 * D)
    joint_sum = lax.psum(scatter(wide), "ctx").astype(F32)
    sums = lax.psum(vecs, ("seq", "ctx", "fsdp"))
    drift = lax.psum(vecs[6], ("seq", "fsdp")).reshape(8, 96)
    drift = lax.all_gather(lax.dynamic_index_in_dim(drift, me, 0, keepdims=False), "ctx", axis=0, tiled=True)
    both = jnp.zeros((4, 2, HF), F32)
    both = lax.dynamic_update_index_in_dim(both, qv[0].reshape(3, HF)[1:3], z, 0)
    both = lax.psum(both, ("seq", "ctx", "fsdp"))
    own = lambda vector: lax.dynamic_slice_in_dim(vector.reshape(-1), 96 * me, 96, 0)
    return (
        outcome[None], tok[None], joint_sum, own(both[:, 1]), own(both[:, 0]), mixer_sum, own(sums[5]), own(sums[3]),
        own(sums[4]), hid_sum, drift, ret_sum, own(sums[2]), own(sums[0]), own(sums[1]),
    )


def specs():
    rows, flat = P(("seq", "fsdp"), None), P(("seq", "fsdp"))
    toks, docs = P("seq", ("ctx", "fsdp"), None), P("seq", ("ctx", "fsdp"))
    ins = (
        toks, docs, rows, flat, flat, rows, flat, flat, flat, rows, flat, rows, flat, flat, flat, toks,
    )
    outs = (
        toks, toks, rows, flat, flat, rows, flat, flat, flat, rows, flat, rows, flat, flat, flat,
    )
    return ins, outs


def solution(mesh):
    ins, outs = specs()
    small_slice = mesh.shape["ctx"] == 4 and mesh.shape["fsdp"] == 4 and mesh.shape["seq"] == 2
    return jax.shard_map(
        shards if small_slice else any_shards, mesh=mesh, in_specs=ins, out_specs=outs, check_vma=False
    )
```
